768 devices in a mesh: dp: 32 (over y_hi, x, core), ctx: 24 (over z, y_lo).
Axes of the slice: x: 4, y: 8 (y_hi: 4, y_lo: 2; y = y_hi * 2 + y_lo), z: 12, core: 2. Of those that a mesh axis runs over, the one named last changes fastest.
Arguments:
- queries: bfloat16 [110592, 2048], P(('dp', 'ctx')), parts along dimension 0, may hold values from -40 to 40
- keys: bfloat16 [110592, 2048], P(('dp', 'ctx')), parts along dimension 0, may hold values from -40 to 40
- values: bfloat16 [110592, 2048], P(('dp', 'ctx')), parts along dimension 0, may hold values from -6 to 6
- span_starts: int32 [192], P('dp'), parts along dimension 0, may hold values from 0 to 3168, as said below
Outputs:
- attended: bfloat16 [110592, 2048], P(('dp', 'ctx')), parts along dimension 0
The draws below stay inside these ranges and needn't reach their ends.
There are 32 independent parts, one for each index of `dp`. The reference program is written for one: setup_inputs(seed, part) draws one part's arguments, and reference() takes and returns one part's arrays. A program takes and returns all parts, laid end to end along the dimension named above; each array names one. Nothing has to cross between parts.
Inputs may be any that keep to these rules, and one draw needn't show every extreme that they name: `span_starts`: starts rise, and the 6 spans of 288 positions lie inside the document without intersecting.
All inputs are finite; a program needn't handle non-finite values.
Results may differ from the reference program's by a relative error of at most 0.0045.
Values may be sent and summed in bfloat16 or wider, within the bound.
No kernel may reach another device: no remote copies, remote signals or barrier semaphores. Data moves between devices by JAX's collectives and lax.ppermute only.
A program may use at most 128 MiB of HBM per device.

```python
import jax
import jax.numpy as jnp
from jax import lax

HEADS = 16
HD = 128
LENGTH = 3456
SPAN = 288
IMAGES = 6


def draw_queries(key, part):
    base = jax.random.truncated_normal(jax.random.fold_in(key, 1), -6.0, 6.0, (LENGTH, HEADS * HD), jnp.float32)
    return base.astype(jnp.bfloat16)


def draw_keys(key, part):
    base = jax.random.truncated_normal(jax.random.fold_in(key, 2), -6.0, 6.0, (LENGTH, HEADS * HD), jnp.float32)
    return base.astype(jnp.bfloat16)


def draw_span_starts(key, part):
    span_count = IMAGES
    spare = LENGTH - span_count * SPAN
    gaps = jnp.sort(jax.random.randint(jax.random.fold_in(key, 4), (span_count,), 0, spare + 1))
    return (jnp.arange(span_count, dtype=jnp.int32) * SPAN + gaps).astype(jnp.int32)


def steps_of(stream_key, extent, split, least, top_value):
    def one(axis_at, parts):
        steps = jax.random.uniform(jax.random.fold_in(jax.random.fold_in(stream_key, 6), axis_at), (parts,), jnp.float32, least / len(split), top_value / len(split))
        return jnp.repeat(jnp.exp(steps), extent[axis_at] // parts).reshape((-1,) + (1,) * (len(extent) - axis_at - 1))

    level = one(*split[0])
    for cut in split[1:]:
        level = level * one(*cut)
    return level


def gaussian(own_key, dims, scale, limit, cuts=(), kind=jnp.bfloat16):
    entries = jax.random.normal(own_key, dims, jnp.float32) * scale
    if len(cuts) > 0:
        entries = steps_of(own_key, dims, cuts, -0.22, 0.18) * entries
    return jnp.clip(entries, min=-limit, max=limit).astype(kind)


def setup_inputs(seed: int = 0, part: int = 0) -> dict:
    key_of = jax.random.split(jax.random.key(seed), 5)
    own_keys = jax.random.split(jax.random.fold_in(key_of[4], part), 5)
    return {
        "queries": draw_queries(jax.random.fold_in(jax.random.fold_in(key_of[4], part), 71), part),
        "keys": draw_keys(jax.random.fold_in(jax.random.fold_in(key_of[4], part), 71), part),
        "values": gaussian(own_keys[2], (LENGTH, HEADS * HD), 1.0, 6.0, ((0, 24),)),
        "span_starts": draw_span_starts(jax.random.fold_in(jax.random.fold_in(key_of[4], part), 71), part),
    }


def span_number(positions, span_starts):
    span_count = span_starts.shape[0]
    inside = (positions[:, None] >= span_starts[None, :]) & (positions[:, None] < span_starts[None, :] + SPAN)
    labels = (jnp.arange(span_count, dtype=jnp.int32) + 1).astype(jnp.int32)
    return jnp.sum(jnp.where(inside, labels[None, :], 0), axis=1).astype(jnp.int32)


def reference(queries, keys, values, span_starts):
    positions = jnp.arange(LENGTH, dtype=jnp.int32)
    span_id = span_number(positions, span_starts)
    visible = (positions[None, :] <= positions[:, None]) | ((span_id[:, None] == span_id[None, :]) & (span_id[:, None] > 0))
    score_scale = HD ** -0.5
    query_heads = queries.reshape(LENGTH, HEADS, HD).transpose(1, 0, 2)
    key_heads = keys.reshape(LENGTH, HEADS, HD).transpose(1, 0, 2)
    value_heads = values.reshape(LENGTH, HEADS, HD).transpose(1, 0, 2)

    def one_head(operands):
        query_h, key_h, value_h = operands
        scores = jnp.dot(query_h, key_h.T, preferred_element_type=jnp.float32) * score_scale
        masked = jnp.where(visible, scores, -jnp.inf)
        row_max = jnp.max(masked, axis=1, keepdims=True)
        weights = jnp.where(visible, jnp.exp(scores - row_max), 0.0)
        total = jnp.sum(weights, axis=1, keepdims=True)
        return jnp.dot(weights.astype(jnp.bfloat16), value_h, preferred_element_type=jnp.float32) / total

    result = lax.map(one_head, (query_heads, key_heads, value_heads))
    return result.transpose(1, 0, 2).reshape(LENGTH, HEADS * HD).astype(jnp.bfloat16)
```

```python
import functools

import jax
import jax.numpy as jnp
from jax import lax
from jax.experimental import pallas as pl
from jax.experimental.pallas import tpu as pltpu
from jax.sharding import PartitionSpec as P

HEADS = 16
HD = 128
SPAN = 288
LOW = -1e30
GAIN = HD ** -0.5 * 1.4426950408889634

VMEM = pl.BlockSpec(memory_space=pltpu.VMEM)
SMEM = pl.BlockSpec(memory_space=pltpu.SMEM)


def head_of(slot):
    return slot // 3 * 2 + (slot % 3 == 2)


def pack_kernel(q_ref, k_ref, v_ref, out_ref):
    for slot in range(out_ref.shape[0]):
        cols = pl.ds(head_of(slot) * HD, HD)
        for part, ref in enumerate((q_ref, k_ref, v_ref)):
            out_ref[slot, :, part * HD : (part + 1) * HD] = ref[:, cols]


def unpack_kernel(in_ref, out_ref):
    for slot in range(in_ref.shape[0]):
        if slot % 3 != 1:
            out_ref[:, head_of(slot) * HD : (head_of(slot) + 1) * HD] = in_ref[slot]


def attend_kernel(starts_ref, qkv_ref, out_ref, acc_ref, top_ref, sum_ref, lim_ref, *, rows, keys, sub):
    length = qkv_ref.shape[0]
    spans = starts_ref.shape[0]
    groups = rows // sub
    lanes = 128
    columns = keys // lanes

    def query_block(block, carry):
        first = pl.multiple_of(block * rows, rows)
        last = first + rows - 1
        reach = last + 1
        pos = first + lax.broadcasted_iota(jnp.int32, (rows, lanes), 0)
        limit = pos + 1
        for i in range(spans):
            start = starts_ref[i]
            end = start + SPAN
            reach = jnp.where((start <= last) & (end > first), jnp.maximum(reach, end), reach)
            limit = jnp.where((pos >= start) & (pos < end), end, limit)
        lim_ref[...] = limit
        top_ref[...] = jnp.full_like(top_ref, LOW)
        sum_ref[...] = jnp.zeros_like(sum_ref)
        acc_ref[...] = jnp.zeros_like(acc_ref)

        def tile(number, masked):
            key0 = pl.multiple_of(number * keys, keys)
            key = qkv_ref[pl.ds(key0, keys), HD : 2 * HD]
            value = qkv_ref[pl.ds(key0, keys), 2 * HD :]

            def score(g):
                query = qkv_ref[pl.ds(first + g * sub, sub), :HD]
                return lax.dot_general(
                    query, key, (((1,), (1,)), ((), ())), preferred_element_type=jnp.float32
                )

            def weights(g, scores):
                at = pl.ds(g * sub, sub)
                parts = [scores[:, j * lanes : (j + 1) * lanes] for j in range(columns)]
                if masked:
                    room = lim_ref[at, :] - key0
                    lane = lax.broadcasted_iota(jnp.int32, (sub, lanes), 1)
                    parts = [jnp.where(lane + j * lanes < room, x, LOW) for j, x in enumerate(parts)]
                old = top_ref[at, :]
                top = functools.reduce(jnp.maximum, parts)
                new = jnp.maximum(old, jnp.max(top, axis=1, keepdims=True))
                fade = jnp.exp2((old - new) * GAIN)
                parts = [jnp.exp2((x - new) * GAIN) for x in parts]
                sum_ref[at, :] = sum_ref[at, :] * fade + functools.reduce(jnp.add, parts)
                top_ref[at, :] = new
                return fade, jnp.concatenate([x.astype(jnp.bfloat16) for x in parts], axis=1)

            def weigh(g, fade, low):
                at = pl.ds(g * sub, sub)
                product = jnp.dot(low, value, preferred_element_type=jnp.float32)
                acc_ref[at, :] = acc_ref[at, :] * fade + product

            scores = {g: score(g) for g in range(min(2, groups))}
            pending = None
            for g in range(groups):
                if g + 2 < groups:
                    scores[g + 2] = score(g + 2)
                current = (g, *weights(g, scores.pop(g)))
                if pending is not None:
                    weigh(*pending)
                pending = current
            weigh(*pending)

        def plain(number, carry):
            tile(number, False)
            return carry

        def masked(number, carry):
            tile(number, True)
            return carry

        full = (first + 1) // keys
        lax.fori_loop(0, full, plain, 0)
        lax.fori_loop(full, (reach + keys - 1) // keys, masked, 0)
        total = jnp.sum(sum_ref[...], axis=1, keepdims=True)
        out_ref[pl.ds(first, rows), :] = (acc_ref[...] / total).astype(out_ref.dtype)
        return carry

    lax.fori_loop(0, length // rows, query_block, 0)


def attend(starts, qkv, rows, keys, sub):
    length = qkv.shape[0]
    return pl.pallas_call(
        functools.partial(attend_kernel, rows=rows, keys=keys, sub=sub),
        out_shape=jax.ShapeDtypeStruct((length, HD), jnp.bfloat16),
        in_specs=[SMEM, VMEM],
        out_specs=VMEM,
        scratch_shapes=[
            pltpu.VMEM((rows, HD), jnp.float32),
            pltpu.VMEM((rows, 128), jnp.float32),
            pltpu.VMEM((rows, 128), jnp.float32),
            pltpu.VMEM((rows, 128), jnp.int32),
        ],
        cost_estimate=pl.CostEstimate(
            flops=2 * length * length * HD,
            bytes_accessed=4 * length * HD * 2,
            transcendentals=length * length // 2,
        ),
        name="attend",
    )(starts, qkv)


def body(queries, keys, values, span_starts):
    rows = queries.shape[0]
    width = queries.shape[1]
    devices = lax.axis_size("ctx")
    packed = pl.pallas_call(
        pack_kernel,
        out_shape=jax.ShapeDtypeStruct((devices, rows, 3 * HD), queries.dtype),
        in_specs=[VMEM] * 3,
        out_specs=VMEM,
        name="pack",
    )(queries, keys, values)
    gathered = lax.all_to_all(packed, "ctx", 0, 0)
    qkv = gathered.reshape(devices * rows, 3 * HD)
    attended = attend(span_starts, qkv, 1152, 1152, 128)
    returned = lax.all_to_all(attended.reshape(devices, rows, HD), "ctx", 0, 0)
    return pl.pallas_call(
        unpack_kernel,
        out_shape=jax.ShapeDtypeStruct((rows, width), queries.dtype),
        in_specs=[VMEM],
        out_specs=VMEM,
        name="unpack",
    )(returned)


def solution(mesh):
    placed = (P(("dp", "ctx"), None), P(("dp", "ctx"), None), P(("dp", "ctx"), None), P("dp"))
    return jax.shard_map(
        body, mesh=mesh, in_specs=placed, out_specs=P(("dp", "ctx"), None), check_vma=False
    )
```

```python
import functools

import jax
import jax.numpy as jnp
from jax import lax
from jax.experimental import pallas as pl
from jax.experimental.pallas import tpu as pltpu
from jax.sharding import PartitionSpec as P


HD = 128
SPAN = 288
LANES = 128
LOW = -1e30
SUB = 192
GAIN = HD ** -0.5 * 1.4426950408889634
OUTER_LOW, RELAY, OUTER_HIGH = 0, 1, 2

VMEM = pl.BlockSpec(memory_space=pltpu.VMEM)
ANY = pl.BlockSpec(memory_space=pl.ANY)
HBM = pl.BlockSpec(memory_space=pltpu.HBM)
SMEM = pl.BlockSpec(memory_space=pltpu.SMEM)


def parity():
    return lax.rem(lax.axis_index("dp"), 2)


def pack_kernel(q_ref, k_ref, v_ref, out_ref, sem):
    shift = parity()
    planes = out_ref.shape[0] // 2
    copies = []
    for plane in range(planes):
        for side in range(2):
            slot = 2 * lax.rem(plane + shift, planes) + side
            head = (plane // 3 * 2 + side) * 2
            low, high = pl.ds(head * HD, HD), pl.ds((head + 1) * HD, HD)
            if plane % 3 == RELAY:
                parts = (q_ref, low), (q_ref, high)
            elif plane % 3 == OUTER_LOW:
                parts = (k_ref, low), (v_ref, low)
            else:
                parts = (k_ref, high), (v_ref, high)
            for at, (ref, columns) in enumerate(parts):
                source = ref.at[:, columns]
                target = out_ref.at[slot, :, pl.ds(at * HD, HD)]
                copies.append(pltpu.make_async_copy(source, target, sem.at[len(copies)]))
    for copy in copies:
        copy.start()
    for copy in copies:
        copy.wait()


def unpack_kernel(in_ref, out_ref, sem):
    shift = parity()
    planes = in_ref.shape[0] // 2
    own = in_ref.shape[1]
    half = own // 2
    copies = []

    def move(source, target):
        copies.append(pltpu.make_async_copy(source, target, sem.at[len(copies)]))

    for plane in range(planes):
        for side in range(2):
            slot = 2 * lax.rem(plane + shift, planes) + side
            head = (plane // 3 * 2 + side) * 2
            low, high = pl.ds(head * HD, HD), pl.ds((head + 1) * HD, HD)
            if plane % 3 == OUTER_LOW:
                move(in_ref.at[slot], out_ref.at[pl.ds(0, own), low])
            elif plane % 3 == OUTER_HIGH:
                move(in_ref.at[slot], out_ref.at[pl.ds(0, own), high])
            else:
                move(in_ref.at[slot, pl.ds(0, half)], out_ref.at[pl.ds(own, half), low])
                move(in_ref.at[slot, pl.ds(half, half)], out_ref.at[pl.ds(own, half), high])
    for copy in copies:
        copy.start()
    for copy in copies:
        copy.wait()


def role():
    planes = lax.axis_size("ctx") // 2
    return lax.rem(lax.axis_index("ctx") // 2 + planes - parity(), 3)


def attend_kernel(starts_ref, low_ref, high_ref, kv_ref, out_ref, lim_ref, *, stride, offset, sub):
    length = kv_ref.shape[0]
    rows = low_ref.shape[0]
    sources = length // stride
    share = rows // sources
    here = role()
    is_high = here == OUTER_HIGH

    def position(source):
        return source * stride + offset + lax.broadcasted_iota(jnp.int32, (share, LANES), 0)

    def limits():
        for source in range(sources):
            lim_ref[pl.ds(source * share, share), :] = position(source) + 1
        for i in range(starts_ref.shape[0]):
            start = starts_ref[i]
            end = start + SPAN
            for step in range((SPAN + stride - 2) // stride + 1):
                source = jnp.minimum(start // stride + step, sources - 1)
                at = pl.ds(pl.multiple_of(source * share, 16), share)
                pos = position(source)
                lim_ref[at, :] = jnp.where((pos >= start) & (pos < end), end, lim_ref[at, :])

    def width(g):
        last = ((g + 1) * sub // share - 1) * stride + offset + share - 1
        return min(-(-(last + SPAN) // LANES) * LANES, length)

    def score(g):
        at = pl.ds(g * sub, sub)
        query = jnp.where(is_high, high_ref[at, :], low_ref[at, :])
        key = kv_ref[: width(g), :HD]
        return lax.dot_general(
            query, key, (((1,), (1,)), ((), ())), preferred_element_type=jnp.float32
        )

    def weights(g, scores):
        at = pl.ds(g * sub, sub)
        parts = [scores[:, j * LANES : (j + 1) * LANES] for j in range(width(g) // LANES)]
        clear = (g * sub // share * stride + offset + 1) // LANES
        room = lim_ref[at, :]
        lane = lax.broadcasted_iota(jnp.int32, (sub, LANES), 1)
        parts = [
            x if j < clear else jnp.where(lane + j * LANES < room, x, LOW)
            for j, x in enumerate(parts)
        ]
        top = jnp.max(functools.reduce(jnp.maximum, parts), axis=1, keepdims=True)
        parts = [jnp.exp2((x - top) * GAIN) for x in parts]
        total = jnp.sum(functools.reduce(jnp.add, parts), axis=1, keepdims=True)
        return total, jnp.concatenate([x.astype(jnp.bfloat16) for x in parts], axis=1)

    def weigh(g, total, low):
        product = jnp.dot(low, kv_ref[: width(g), HD:], preferred_element_type=jnp.float32)
        out_ref[pl.ds(g * sub, sub), :] = (product / total).astype(out_ref.dtype)

    @pl.when(here != RELAY)
    def _():
        limits()
        groups = rows // sub
        scores = score(0)
        pending = None
        for g in range(groups):
            ahead = score(g + 1) if g + 1 < groups else None
            current = (g, *weights(g, scores))
            scores = ahead
            if pending is not None:
                weigh(*pending)
            pending = current
        weigh(*pending)

    @pl.when(here == RELAY)
    def _():
        out_ref[...] = jnp.zeros_like(out_ref)


def attend(starts, low, high, kv, stride, offset):
    rows = low.shape[0]
    return pl.pallas_call(
        functools.partial(attend_kernel, stride=stride, offset=offset, sub=SUB),
        out_shape=jax.ShapeDtypeStruct((rows, HD), jnp.bfloat16),
        in_specs=[SMEM, VMEM, VMEM, VMEM],
        out_specs=VMEM,
        scratch_shapes=[pltpu.VMEM((rows, LANES), jnp.int32)],
        cost_estimate=pl.CostEstimate(
            flops=2 * rows * kv.shape[0] * HD,
            bytes_accessed=(2 * rows + 2 * kv.shape[0]) * HD * 2,
            transcendentals=rows * kv.shape[0] // 2,
        ),
        compiler_params=pltpu.CompilerParams(vmem_limit_bytes=40 << 20),
        name="attend",
    )(starts, low, high, kv)


def merge_kernel(own_ref, low_ref, high_ref, out_ref, sem):
    half = out_ref.shape[1] // 2

    @pl.when(role() == RELAY)
    def _():
        copies = [
            pltpu.make_async_copy(ref, out_ref.at[:, pl.ds(at * half, half)], sem.at[at])
            for at, ref in enumerate((low_ref, high_ref))
        ]
        for copy in copies:
            copy.start()
        for copy in copies:
            copy.wait()


def body(queries, keys, values, span_starts):
    rows = queries.shape[0]
    width = queries.shape[1]
    devices = lax.axis_size("ctx")
    docs = lax.axis_size("dp")
    planes = devices // 2
    own = rows // 3 * 2
    packed = pl.pallas_call(
        pack_kernel,
        out_shape=jax.ShapeDtypeStruct((devices, rows, 2 * HD), queries.dtype),
        in_specs=[HBM] * 3,
        out_specs=VMEM,
        scratch_shapes=[pltpu.SemaphoreType.DMA((2 * devices,))],
        compiler_params=pltpu.CompilerParams(vmem_limit_bytes=62 << 20),
        name="pack",
    )(queries, keys, values)
    gathered = lax.all_to_all(packed, "ctx", 0, 0)
    kv = gathered.reshape(devices * rows, 2 * HD)

    def relay(block, step, back=False):
        pairs = []
        for doc in range(docs):
            for plane in range(RELAY, planes, 3):
                for side in range(2):
                    middle = 2 * ((plane + doc % 2) % planes) + side
                    outer = 2 * ((plane + step + doc % 2) % planes) + side
                    pair = (doc * devices + middle, doc * devices + outer)
                    pairs.append(pair[::-1] if back else pair)
        return lax.ppermute(block, ("dp", "ctx"), pairs)

    def queries_of(start, stop):
        parts = [gathered[:, start:stop, at * HD : (at + 1) * HD] for at in range(2)]
        sent = [relay(part, step) for part, step in zip(parts, (-1, 1))]
        return [part.reshape(-1, HD) for part in sent]

    tail = queries_of(own, rows)
    head = queries_of(0, own)
    lent = attend(span_starts, *tail, kv, rows, own).reshape(devices, rows - own, HD)
    lent = [relay(lent, step, True) for step in (-1, 1)]
    kept = attend(span_starts, *head, kv, rows, 0).reshape(devices, own, HD)
    shared = pl.pallas_call(
        merge_kernel,
        out_shape=jax.ShapeDtypeStruct(kept.shape, kept.dtype),
        in_specs=[ANY] * 3,
        out_specs=ANY,
        input_output_aliases={0: 0},
        scratch_shapes=[pltpu.SemaphoreType.DMA((2,))],
        compiler_params=pltpu.CompilerParams(vmem_limit_bytes=8 << 20),
        name="merge",
    )(kept, *lent)
    returned = lax.all_to_all(shared, "ctx", 0, 0)
    return pl.pallas_call(
        unpack_kernel,
        out_shape=jax.ShapeDtypeStruct((rows, width), queries.dtype),
        in_specs=[VMEM],
        out_specs=ANY,
        scratch_shapes=[pltpu.SemaphoreType.DMA((2 * devices,))],
        compiler_params=pltpu.CompilerParams(vmem_limit_bytes=8 << 20),
        name="unpack",
    )(returned)


def solution(mesh):
    placed = (P(("dp", "ctx"), None), P(("dp", "ctx"), None), P(("dp", "ctx"), None), P("dp"))
    return jax.shard_map(
        body, mesh=mesh, in_specs=placed, out_specs=P(("dp", "ctx"), None), check_vma=False
    )
```

```python
import functools

import jax
import jax.numpy as jnp
from jax import lax
from jax.experimental import pallas as pl
from jax.experimental.pallas import tpu as pltpu
from jax.sharding import PartitionSpec as P


HD = 128
SPAN = 288
LANES = 128
LOW = -1e30
SUB = 192
GAIN = HD ** -0.5 * 1.4426950408889634
OUTER_LOW, RELAY, OUTER_HIGH = 0, 1, 2

VMEM = pl.BlockSpec(memory_space=pltpu.VMEM)
ANY = pl.BlockSpec(memory_space=pl.ANY)
HBM = pl.BlockSpec(memory_space=pltpu.HBM)
SMEM = pl.BlockSpec(memory_space=pltpu.SMEM)


def parity():
    return lax.rem(lax.axis_index("dp"), 2)


def pack_kernel(q_ref, k_ref, v_ref, out_ref, sem):
    shift = parity()
    planes = out_ref.shape[0] // 2
    copies = []
    for plane in range(planes):
        for side in range(2):
            slot = 2 * lax.rem(plane + shift, planes) + side
            head = (plane // 3 * 2 + side) * 2
            low, high = pl.ds(head * HD, HD), pl.ds((head + 1) * HD, HD)
            if plane % 3 == RELAY:
                parts = (q_ref, low), (q_ref, high)
            elif plane % 3 == OUTER_LOW:
                parts = (k_ref, low), (v_ref, low)
            else:
                parts = (k_ref, high), (v_ref, high)
            for at, (ref, columns) in enumerate(parts):
                source = ref.at[:, columns]
                target = out_ref.at[slot, :, pl.ds(at * HD, HD)]
                copies.append(pltpu.make_async_copy(source, target, sem.at[len(copies)]))
    for copy in copies:
        copy.start()
    for copy in copies:
        copy.wait()


def unpack_kernel(in_ref, out_ref, sem):
    shift = parity()
    planes = in_ref.shape[0] // 2
    own = in_ref.shape[1]
    half = own // 2
    copies = []

    def move(source, target):
        copies.append(pltpu.make_async_copy(source, target, sem.at[len(copies)]))

    for plane in range(planes):
        for side in range(2):
            slot = 2 * lax.rem(plane + shift, planes) + side
            head = (plane // 3 * 2 + side) * 2
            low, high = pl.ds(head * HD, HD), pl.ds((head + 1) * HD, HD)
            if plane % 3 == OUTER_LOW:
                move(in_ref.at[slot], out_ref.at[pl.ds(0, own), low])
            elif plane % 3 == OUTER_HIGH:
                move(in_ref.at[slot], out_ref.at[pl.ds(0, own), high])
            else:
                move(in_ref.at[slot, pl.ds(0, half)], out_ref.at[pl.ds(own, half), low])
                move(in_ref.at[slot, pl.ds(half, half)], out_ref.at[pl.ds(own, half), high])
    for copy in copies:
        copy.start()
    for copy in copies:
        copy.wait()


def role():
    planes = lax.axis_size("ctx") // 2
    return lax.rem(lax.axis_index("ctx") // 2 + planes - parity(), 3)


def attend_kernel(starts_ref, low_ref, high_ref, kv_ref, out_ref, lim_ref, wide_ref, *, stride, offset, sub):
    length = kv_ref.shape[0]
    rows = low_ref.shape[0]
    sources = length // stride
    share = rows // sources
    here = role()
    is_high = here == OUTER_HIGH

    def position(source):
        return source * stride + offset + lax.broadcasted_iota(jnp.int32, (share, LANES), 0)

    def limits():
        for source in range(sources):
            lim_ref[pl.ds(source * share, share), :] = position(source) + 1
        for i in range(starts_ref.shape[0]):
            start = starts_ref[i]
            end = start + SPAN
            for step in range((SPAN + stride - 2) // stride + 1):
                source = jnp.minimum(start // stride + step, sources - 1)
                at = pl.ds(pl.multiple_of(source * share, 16), share)
                pos = position(source)
                lim_ref[at, :] = jnp.where((pos >= start) & (pos < end), end, lim_ref[at, :])

    def width(g):
        last = ((g + 1) * sub // share - 1) * stride + offset + share - 1
        return min(-(-(last + SPAN) // LANES) * LANES, length)

    def score(g):
        at = pl.ds(g * sub, sub)
        query = jnp.where(is_high, high_ref[at, :], low_ref[at, :])
        key = kv_ref[: width(g), :HD]
        return lax.dot_general(
            query, key, (((1,), (1,)), ((), ())), preferred_element_type=jnp.float32
        )

    def weights(g, scores):
        at = pl.ds(g * sub, sub)
        parts = [scores[:, j * LANES : (j + 1) * LANES] for j in range(width(g) // LANES)]
        clear = (g * sub // share * stride + offset + 1) // LANES
        room = lim_ref[at, :]
        lane = lax.broadcasted_iota(jnp.int32, (sub, LANES), 1)
        parts = [
            x if j < clear else jnp.where(lane + j * LANES < room, x, LOW)
            for j, x in enumerate(parts)
        ]
        top = jnp.max(functools.reduce(jnp.maximum, parts), axis=1, keepdims=True)
        low = [jnp.exp2((x - top) * GAIN).astype(jnp.bfloat16) for x in parts]
        return jnp.concatenate(low, axis=1)

    def weigh(g, low):
        product = jnp.dot(low, wide_ref[: width(g), :], preferred_element_type=jnp.float32)
        out_ref[pl.ds(g * sub, sub), :] = (product[:, :HD] / product[:, HD:]).astype(out_ref.dtype)

    @pl.when(here != RELAY)
    def _():
        limits()
        wide_ref[:, :HD] = kv_ref[:, HD:]
        wide_ref[:, HD:] = jnp.ones((length, HD), jnp.bfloat16)
        groups = rows // sub
        scores = score(0)
        pending = None
        for g in range(groups):
            ahead = score(g + 1) if g + 1 < groups else None
            current = (g, weights(g, scores))
            scores = ahead
            if pending is not None:
                weigh(*pending)
            pending = current
        weigh(*pending)

    @pl.when(here == RELAY)
    def _():
        out_ref[...] = jnp.zeros_like(out_ref)


def attend(starts, low, high, kv, stride, offset):
    rows = low.shape[0]
    return pl.pallas_call(
        functools.partial(attend_kernel, stride=stride, offset=offset, sub=SUB),
        out_shape=jax.ShapeDtypeStruct((rows, HD), jnp.bfloat16),
        in_specs=[SMEM, VMEM, VMEM, VMEM],
        out_specs=VMEM,
        scratch_shapes=[pltpu.VMEM((rows, LANES), jnp.int32), pltpu.VMEM((kv.shape[0], 2 * HD), jnp.bfloat16)],
        cost_estimate=pl.CostEstimate(
            flops=2 * rows * kv.shape[0] * HD,
            bytes_accessed=(2 * rows + 2 * kv.shape[0]) * HD * 2,
            transcendentals=rows * kv.shape[0] // 2,
        ),
        compiler_params=pltpu.CompilerParams(vmem_limit_bytes=40 << 20),
        name="attend",
    )(starts, low, high, kv)


def merge_kernel(own_ref, low_ref, high_ref, out_ref, sem):
    half = out_ref.shape[1] // 2

    @pl.when(role() == RELAY)
    def _():
        copies = [
            pltpu.make_async_copy(ref, out_ref.at[:, pl.ds(at * half, half)], sem.at[at])
            for at, ref in enumerate((low_ref, high_ref))
        ]
        for copy in copies:
            copy.start()
        for copy in copies:
            copy.wait()


def body(queries, keys, values, span_starts):
    rows = queries.shape[0]
    width = queries.shape[1]
    devices = lax.axis_size("ctx")
    docs = lax.axis_size("dp")
    planes = devices // 2
    own = rows // 3 * 2
    packed = pl.pallas_call(
        pack_kernel,
        out_shape=jax.ShapeDtypeStruct((devices, rows, 2 * HD), queries.dtype),
        in_specs=[HBM] * 3,
        out_specs=VMEM,
        scratch_shapes=[pltpu.SemaphoreType.DMA((2 * devices,))],
        compiler_params=pltpu.CompilerParams(vmem_limit_bytes=8 << 20),
        name="pack",
    )(*(pltpu.with_memory_space_constraint(x, pltpu.HBM) for x in (queries, keys, values)))
    gathered = lax.all_to_all(packed, "ctx", 0, 0)
    kv = gathered.reshape(devices * rows, 2 * HD)

    def relay(block, step, back=False):
        pairs = []
        for doc in range(docs):
            for plane in range(RELAY, planes, 3):
                for side in range(2):
                    middle = 2 * ((plane + doc % 2) % planes) + side
                    outer = 2 * ((plane + step + doc % 2) % planes) + side
                    pair = (doc * devices + middle, doc * devices + outer)
                    pairs.append(pair[::-1] if back else pair)
        return lax.ppermute(block, ("dp", "ctx"), pairs)

    def queries_of(start, stop):
        parts = [gathered[:, start:stop, at * HD : (at + 1) * HD] for at in range(2)]
        sent = [relay(part, step) for part, step in zip(parts, (-1, 1))]
        return [part.reshape(-1, HD) for part in sent]

    tail = queries_of(own, rows)
    head = queries_of(0, own)
    lent = attend(span_starts, *tail, kv, rows, own).reshape(devices, rows - own, HD)
    lent = [relay(lent, step, True) for step in (-1, 1)]
    kept = attend(span_starts, *head, kv, rows, 0).reshape(devices, own, HD)
    shared = pl.pallas_call(
        merge_kernel,
        out_shape=jax.ShapeDtypeStruct(kept.shape, kept.dtype),
        in_specs=[ANY] * 3,
        out_specs=ANY,
        input_output_aliases={0: 0},
        scratch_shapes=[pltpu.SemaphoreType.DMA((2,))],
        compiler_params=pltpu.CompilerParams(vmem_limit_bytes=8 << 20),
        name="merge",
    )(kept, *lent)
    returned = lax.all_to_all(shared, "ctx", 0, 0)
    return pl.pallas_call(
        unpack_kernel,
        out_shape=jax.ShapeDtypeStruct((rows, width), queries.dtype),
        in_specs=[VMEM],
        out_specs=ANY,
        scratch_shapes=[pltpu.SemaphoreType.DMA((2 * devices,))],
        compiler_params=pltpu.CompilerParams(vmem_limit_bytes=8 << 20),
        name="unpack",
    )(returned)


def solution(mesh):
    placed = (P(("dp", "ctx"), None), P(("dp", "ctx"), None), P(("dp", "ctx"), None), P("dp"))
    return jax.shard_map(
        body, mesh=mesh, in_specs=placed, out_specs=P(("dp", "ctx"), None), check_vma=False
    )
```

```python
import functools

import jax
import jax.numpy as jnp
from jax import lax
from jax.experimental import pallas as pl
from jax.experimental.pallas import tpu as pltpu
from jax.sharding import PartitionSpec as P


HD = 128
SPAN = 288
LANES = 128
LOW = -1e30
SUB = 192
GAIN = HD ** -0.5 * 1.4426950408889634
OUTER_LOW, RELAY, OUTER_HIGH = 0, 1, 2

VMEM = pl.BlockSpec(memory_space=pltpu.VMEM)
ANY = pl.BlockSpec(memory_space=pl.ANY)
HBM = pl.BlockSpec(memory_space=pltpu.HBM)
SMEM = pl.BlockSpec(memory_space=pltpu.SMEM)


def parity():
    return lax.rem(lax.axis_index("dp"), 2)


def pack_kernel(q_ref, k_ref, v_ref, out_ref, sem):
    shift = parity()
    planes = out_ref.shape[0] // 2
    copies = []
    for plane in range(planes):
        for side in range(2):
            slot = 2 * lax.rem(plane + shift, planes) + side
            head = (plane // 3 * 2 + side) * 2
            low, high = pl.ds(head * HD, HD), pl.ds((head + 1) * HD, HD)
            if plane % 3 == RELAY:
                parts = (q_ref, low), (q_ref, high)
            elif plane % 3 == OUTER_LOW:
                parts = (k_ref, low), (v_ref, low)
            else:
                parts = (k_ref, high), (v_ref, high)
            for at, (ref, columns) in enumerate(parts):
                source = ref.at[:, columns]
                target = out_ref.at[slot, :, pl.ds(at * HD, HD)]
                copies.append(pltpu.make_async_copy(source, target, sem.at[len(copies)]))
    for copy in copies:
        copy.start()
    for copy in copies:
        copy.wait()


def unpack_kernel(in_ref, out_ref, sem):
    shift = parity()
    planes = in_ref.shape[0] // 2
    own = in_ref.shape[1]
    half = own // 2
    copies = []

    def move(source, target):
        copies.append(pltpu.make_async_copy(source, target, sem.at[len(copies)]))

    for plane in range(planes):
        for side in range(2):
            slot = 2 * lax.rem(plane + shift, planes) + side
            head = (plane // 3 * 2 + side) * 2
            low, high = pl.ds(head * HD, HD), pl.ds((head + 1) * HD, HD)
            if plane % 3 == OUTER_LOW:
                move(in_ref.at[slot], out_ref.at[pl.ds(0, own), low])
            elif plane % 3 == OUTER_HIGH:
                move(in_ref.at[slot], out_ref.at[pl.ds(0, own), high])
            else:
                move(in_ref.at[slot, pl.ds(0, half)], out_ref.at[pl.ds(own, half), low])
                move(in_ref.at[slot, pl.ds(half, half)], out_ref.at[pl.ds(own, half), high])
    for copy in copies:
        copy.start()
    for copy in copies:
        copy.wait()


def role():
    planes = lax.axis_size("ctx") // 2
    return lax.rem(lax.axis_index("ctx") // 2 + planes - parity(), 3)


def prepare_kernel(starts_ref, kv_ref, wide_ref, *lim_refs, stride, offsets):
    length = kv_ref.shape[0]
    sources = length // stride
    wide_ref[:, :HD] = kv_ref[:, HD:]
    wide_ref[:, HD:] = jnp.ones((length, HD), jnp.bfloat16)
    for offset, lim_ref in zip(offsets, lim_refs):
        share = lim_ref.shape[0] // sources

        def position(source):
            return source * stride + offset + lax.broadcasted_iota(jnp.int32, (share, LANES), 0)

        for source in range(sources):
            lim_ref[pl.ds(source * share, share), :] = position(source) + 1
        for i in range(starts_ref.shape[0]):
            start = starts_ref[i]
            end = start + SPAN
            for step in range((SPAN + stride - 2) // stride + 1):
                source = jnp.minimum(start // stride + step, sources - 1)
                at = pl.ds(pl.multiple_of(source * share, 16), share)
                pos = position(source)
                lim_ref[at, :] = jnp.where((pos >= start) & (pos < end), end, lim_ref[at, :])


def attend_kernel(lim_ref, low_ref, high_ref, kv_ref, wide_ref, out_ref, *, stride, offset, sub):
    length = kv_ref.shape[0]
    rows = low_ref.shape[0]
    sources = length // stride
    share = rows // sources
    here = role()
    is_high = here == OUTER_HIGH

    def width(g):
        last = ((g + 1) * sub // share - 1) * stride + offset + share - 1
        return min(-(-(last + SPAN) // LANES) * LANES, length)

    def score(g):
        at = pl.ds(g * sub, sub)
        query = jnp.where(is_high, high_ref[at, :], low_ref[at, :])
        key = kv_ref[: width(g), :HD]
        return lax.dot_general(
            query, key, (((1,), (1,)), ((), ())), preferred_element_type=jnp.float32
        )

    def weights(g, scores):
        at = pl.ds(g * sub, sub)
        parts = [scores[:, j * LANES : (j + 1) * LANES] for j in range(width(g) // LANES)]
        clear = (g * sub // share * stride + offset + 1) // LANES
        room = lim_ref[at, :]
        lane = lax.broadcasted_iota(jnp.int32, (sub, LANES), 1)
        parts = [
            x if j < clear else jnp.where(lane + j * LANES < room, x, LOW)
            for j, x in enumerate(parts)
        ]
        top = jnp.max(functools.reduce(jnp.maximum, parts), axis=1, keepdims=True)
        low = [jnp.exp2((x - top) * GAIN).astype(jnp.bfloat16) for x in parts]
        return jnp.concatenate(low, axis=1)

    def weigh(g, low):
        product = jnp.dot(low, wide_ref[: width(g), :], preferred_element_type=jnp.float32)
        out_ref[pl.ds(g * sub, sub), :] = (product[:, :HD] / product[:, HD:]).astype(out_ref.dtype)

    @pl.when(here != RELAY)
    def _():
        groups = rows // sub
        scores = score(0)
        pending = None
        for g in range(groups):
            ahead = score(g + 1) if g + 1 < groups else None
            current = (g, weights(g, scores))
            scores = ahead
            if pending is not None:
                weigh(*pending)
            pending = current
        weigh(*pending)

    @pl.when(here == RELAY)
    def _():
        out_ref[...] = jnp.zeros_like(out_ref)


def attend(limits, low, high, kv, wide, stride, offset):
    rows = low.shape[0]
    return pl.pallas_call(
        functools.partial(attend_kernel, stride=stride, offset=offset, sub=SUB),
        out_shape=jax.ShapeDtypeStruct((rows, HD), jnp.bfloat16),
        in_specs=[VMEM] * 5,
        out_specs=VMEM,
        cost_estimate=pl.CostEstimate(
            flops=2 * rows * kv.shape[0] * HD,
            bytes_accessed=(2 * rows + 2 * kv.shape[0]) * HD * 2,
            transcendentals=rows * kv.shape[0] // 2,
        ),
        compiler_params=pltpu.CompilerParams(vmem_limit_bytes=40 << 20),
        name="attend",
    )(limits, low, high, kv, wide)


def merge_kernel(own_ref, low_ref, high_ref, out_ref, sem):
    half = out_ref.shape[1] // 2

    @pl.when(role() == RELAY)
    def _():
        copies = [
            pltpu.make_async_copy(ref, out_ref.at[:, pl.ds(at * half, half)], sem.at[at])
            for at, ref in enumerate((low_ref, high_ref))
        ]
        for copy in copies:
            copy.start()
        for copy in copies:
            copy.wait()


def body(queries, keys, values, span_starts):
    rows = queries.shape[0]
    width = queries.shape[1]
    devices = lax.axis_size("ctx")
    docs = lax.axis_size("dp")
    planes = devices // 2
    own = rows // 3 * 2
    packed = pl.pallas_call(
        pack_kernel,
        out_shape=jax.ShapeDtypeStruct((devices, rows, 2 * HD), queries.dtype),
        in_specs=[HBM] * 3,
        out_specs=VMEM,
        scratch_shapes=[pltpu.SemaphoreType.DMA((2 * devices,))],
        compiler_params=pltpu.CompilerParams(vmem_limit_bytes=8 << 20),
        name="pack",
    )(*(pltpu.with_memory_space_constraint(x, pltpu.HBM) for x in (queries, keys, values)))
    gathered = lax.all_to_all(packed, "ctx", 0, 0)
    kv = gathered.reshape(devices * rows, 2 * HD)

    def relay(block, step, back=False):
        pairs = []
        for doc in range(docs):
            for plane in range(RELAY, planes, 3):
                for side in range(2):
                    middle = 2 * ((plane + doc % 2) % planes) + side
                    outer = 2 * ((plane + step + doc % 2) % planes) + side
                    pair = (doc * devices + middle, doc * devices + outer)
                    pairs.append(pair[::-1] if back else pair)
        return lax.ppermute(block, ("dp", "ctx"), pairs)

    def queries_of(start, stop):
        parts = [gathered[:, start:stop, at * HD : (at + 1) * HD] for at in range(2)]
        sent = [relay(part, step) for part, step in zip(parts, (-1, 1))]
        return [part.reshape(-1, HD) for part in sent]

    tail = queries_of(own, rows)
    head = queries_of(0, own)
    wide, tail_limits, head_limits = pl.pallas_call(
        functools.partial(prepare_kernel, stride=rows, offsets=(own, 0)),
        out_shape=(
            jax.ShapeDtypeStruct(kv.shape, kv.dtype),
            jax.ShapeDtypeStruct((devices * (rows - own), LANES), jnp.int32),
            jax.ShapeDtypeStruct((devices * own, LANES), jnp.int32),
        ),
        in_specs=[SMEM, VMEM],
        out_specs=(VMEM,) * 3,
        compiler_params=pltpu.CompilerParams(vmem_limit_bytes=8 << 20),
        name="prepare",
    )(span_starts, kv)
    lent = attend(tail_limits, *tail, kv, wide, rows, own).reshape(devices, rows - own, HD)
    lent = [relay(lent, step, True) for step in (-1, 1)]
    kept = attend(head_limits, *head, kv, wide, rows, 0).reshape(devices, own, HD)
    shared = pl.pallas_call(
        merge_kernel,
        out_shape=jax.ShapeDtypeStruct(kept.shape, kept.dtype),
        in_specs=[ANY] * 3,
        out_specs=ANY,
        input_output_aliases={0: 0},
        scratch_shapes=[pltpu.SemaphoreType.DMA((2,))],
        compiler_params=pltpu.CompilerParams(vmem_limit_bytes=8 << 20),
        name="merge",
    )(kept, *lent)
    returned = lax.all_to_all(shared, "ctx", 0, 0)
    return pl.pallas_call(
        unpack_kernel,
        out_shape=jax.ShapeDtypeStruct((rows, width), queries.dtype),
        in_specs=[VMEM],
        out_specs=ANY,
        scratch_shapes=[pltpu.SemaphoreType.DMA((2 * devices,))],
        compiler_params=pltpu.CompilerParams(vmem_limit_bytes=8 << 20),
        name="unpack",
    )(returned)


def solution(mesh):
    placed = (P(("dp", "ctx"), None), P(("dp", "ctx"), None), P(("dp", "ctx"), None), P("dp"))
    return jax.shard_map(
        body, mesh=mesh, in_specs=placed, out_specs=P(("dp", "ctx"), None), check_vma=False
    )
```
